32 devices in a mesh: slide: 4 (over x, core), rows: 8 (over z, y).
Axes of the slice: x: 2, y: 2, z: 4, core: 2. Of those that a mesh axis runs over, the one named last changes fastest.
Arguments:
- features: bfloat16 [4, 192, 256, 128], P('slide', None, 'rows'), may hold values from -6 to 6
- depth_kernel: float32 [192, 49], replicated, may hold values from -0.875 to 0.875
- depth_bias: float32 [192], replicated, may hold values from -4 to 4
- norm_gain: float32 [192], replicated, may hold values from 0.1 to 1.9
- norm_bias: float32 [192], replicated, may hold values from -3 to 3
- up_weight: bfloat16 [192, 768], replicated, may hold values from -0.4375 to 0.4375
- up_bias: float32 [768], replicated, may hold values from -3 to 3
- down_weight: bfloat16 [768, 192], replicated, may hold values from -0.21875 to 0.21875
- down_bias: float32 [192], replicated, may hold values from -4 to 4
- layer_scale: float32 [192], replicated, may hold values from 0.2 to 1
- tissue: int32 [4, 8, 4], P('slide', 'rows'), may hold values 0 or 1
- aggregator_order: int32 [4, 32], P('slide'), may hold values from 0 to 31, each once within a row
- tile_cotangent: bfloat16 [4, 32, 192], P('slide', 'rows'), may hold values from -6 to 6
Outputs:
- embedding: float32 [4, 32, 192], P('slide', 'rows')
- input_grad: bfloat16 [4, 192, 256, 128], P('slide', None, 'rows')
- grad_up: float32 [192, 768], replicated
- grad_down: float32 [768, 192], replicated
- grad_kernel: float32 [192, 49], replicated
The draws below stay inside these ranges and needn't reach their ends.
Inputs may be any that keep to these rules, and one draw needn't show every extreme that they name: `aggregator_order`: each slide's row is a permutation of the 32 positions.
All inputs are finite; a program needn't handle non-finite values. No bound on the sum of `tissue` on one device may be relied on, other than what follows from the above.
Results may differ from the reference program's by a relative error of at most 0.0064.
Values may be sent and summed in bfloat16 or wider, within the bound.
A program may use at most 128 MiB of HBM per device.

```python
import math
import jax
import jax.numpy as jnp
from jax import lax

C = 192
HID = 768
TILE = 32
WIDTH = 128
SLIDES = 4
HEIGHT = 256
TILES_DEV = 4
TILES = 32


def plant(entries, stream_key, least, top_value):
    place = [jax.random.randint(jax.random.fold_in(stream_key, axis), (), 0, length) for axis, length in enumerate(entries.shape)]
    longest = entries.shape.index(max(entries.shape))
    beside = place[:longest] + [(place[longest] + 1) % entries.shape[longest]] + place[longest + 1:]
    return entries.at[tuple(place)].set(least).at[tuple(beside)].set(top_value)


def steps_of(own_key, shape, split, least, high):
    gain = 1.0
    for dim, parts in split:
        heights = jax.random.uniform(jax.random.fold_in(jax.random.fold_in(own_key, 6), dim), (parts,), jnp.float32, least / len(split), high / len(split))
        gain = gain * jnp.repeat(jnp.exp(heights), shape[dim] // parts).reshape((-1,) + (1,) * (len(shape) - 1 - dim))
    return gain


def normal_values(stream_key, dims, spread, limit, shards=(), held_as=jnp.bfloat16):
    result = spread * jax.random.normal(stream_key, dims, jnp.float32)
    if shards:
        result = result * steps_of(stream_key, dims, shards, -0.22, 0.18)
    return jnp.clip(result, -limit, limit).astype(held_as)


def setup_inputs(seed: int = 0) -> dict:
    key_list = jax.random.split(jax.random.key(seed), 14)
    return {
        "features": normal_values(key_list[0], (SLIDES, C, HEIGHT, WIDTH), 1.0, 6.0, ((0, 4), (2, 8))),
        "depth_kernel": normal_values(key_list[1], (C, 49), 49 ** -0.5, 0.875, (), jnp.float32),
        "depth_bias": normal_values(key_list[2], (C,), 1.0, 4.0, (), jnp.float32),
        "norm_gain": jnp.clip(1.0 + 0.18 * jax.random.normal(key_list[3], (C,), jnp.float32), 0.1, 1.9),
        "norm_bias": normal_values(key_list[4], (C,), 0.5, 3.0, (), jnp.float32),
        "up_weight": normal_values(key_list[5], (C, HID), C ** -0.5, 0.4375),
        "up_bias": normal_values(key_list[6], (HID,), 0.5, 3.0, (), jnp.float32),
        "down_weight": normal_values(key_list[7], (HID, C), HID ** -0.5, 0.21875),
        "down_bias": normal_values(key_list[8], (C,), 1.0, 4.0, (), jnp.float32),
        "layer_scale": jnp.clip(jnp.exp(jax.random.uniform(key_list[9], (C,), jnp.float32, math.log(0.2), math.log(1.0))), 0.2, 1.0),
        "tissue": plant((jax.random.randint(key_list[10], (SLIDES, HEIGHT // TILE, TILES_DEV), 0, 3) < 2).astype(jnp.int32), jax.random.fold_in(key_list[10], 1), 0, 1),
        "aggregator_order": jax.vmap(lambda own: jax.random.permutation(own, TILES))(jax.random.split(key_list[11], SLIDES)).reshape((SLIDES, TILES)).astype(jnp.int32),
        "tile_cotangent": normal_values(key_list[12], (SLIDES, TILES, C), 1.0, 6.0, ((0, 4), (1, 8))),
    }


def depthwise(source, kernel, height, across, mirrored):
    channels = source.shape[0]
    total = jnp.zeros((channels, height, across), jnp.float32)
    for position in range(49):
        row_start = position // 7
        col_start = position % 7
        if mirrored:
            row_start = 6 - row_start
            col_start = 6 - col_start
        window = lax.slice(source, (0, row_start, col_start), (channels, row_start + height, col_start + across))
        total = total + kernel[:, position][:, None, None] * window.astype(jnp.float32)
    return total

def gelu_exact(values):
    return 0.5 * values * (1.0 + jax.scipy.special.erf(values * 0.7071067811865476))

def gelu_slope(values):
    cumulative = 0.5 * (1.0 + jax.scipy.special.erf(values * 0.7071067811865476))
    density = jnp.exp(-0.5 * values * values) * 0.3989422804014327
    return cumulative + values * density

def block_pass(conv_flat, image_flat, pixel_mask, pixel_cotangent, norm_gain, norm_bias, up_weight, up_bias, down_weight, down_bias, layer_scale):
    average = lax.optimization_barrier(jnp.mean(conv_flat, axis=0, keepdims=True))
    centered = conv_flat - average
    variance = lax.optimization_barrier(jnp.mean(centered * centered, axis=0, keepdims=True))
    reciprocal = lax.rsqrt(variance + 1e-06)
    standard = centered * reciprocal
    normed = (standard * norm_gain[:, None] + norm_bias[:, None]).astype(jnp.bfloat16)
    activation_in = jnp.dot(up_weight.T, normed, preferred_element_type=jnp.float32) + up_bias[:, None]
    hidden = gelu_exact(activation_in).astype(jnp.bfloat16)
    branch = jnp.dot(down_weight.T, hidden, preferred_element_type=jnp.float32) + down_bias[:, None]
    scaled_mask = pixel_mask[None, :] * layer_scale[:, None]
    output = image_flat.astype(jnp.float32) + scaled_mask * branch
    grad_branch = (scaled_mask * pixel_cotangent).astype(jnp.bfloat16)
    grad_hidden = jnp.dot(down_weight, grad_branch, preferred_element_type=jnp.float32)
    grad_activation = (grad_hidden * gelu_slope(activation_in)).astype(jnp.bfloat16)
    grad_normed = jnp.dot(up_weight, grad_activation, preferred_element_type=jnp.float32)
    grad_standard = grad_normed * norm_gain[:, None]
    grad_conv = reciprocal * (grad_standard - lax.optimization_barrier(jnp.mean(grad_standard, axis=0, keepdims=True)) - standard * lax.optimization_barrier(jnp.mean(grad_standard * standard, axis=0, keepdims=True)))
    grad_conv = grad_conv.astype(jnp.bfloat16)
    up_term = jnp.dot(normed, grad_activation.T, preferred_element_type=jnp.float32)
    down_term = jnp.dot(grad_branch, hidden.T, preferred_element_type=jnp.float32)
    return (output, grad_conv, up_term, down_term)

def reference(features, depth_kernel, depth_bias, norm_gain, norm_bias, up_weight, up_bias, down_weight, down_bias, layer_scale, tissue, aggregator_order, tile_cotangent):
    loss_norm = 1.0 / math.sqrt(SLIDES * HEIGHT * WIDTH)
    tile_rows = HEIGHT // TILE
    block_pixels = TILE * WIDTH

    def slide_pass(inputs):
        pixels_in, tissue_map, order, cotangent = inputs
        extended = jnp.pad(pixels_in, ((0, 0), (3, 3), (3, 3)))
        convolved = depthwise(extended, depth_kernel, HEIGHT, WIDTH, False) + depth_bias[:, None, None]
        wanted = jnp.take(cotangent, order.astype(jnp.int32), axis=0).astype(jnp.float32)
        wanted = wanted.reshape(tile_rows, TILES_DEV, C)
        masks = tissue_map.astype(jnp.float32)
        conv_rows = convolved.reshape(C, tile_rows, block_pixels).transpose(1, 0, 2)
        image_rows = pixels_in.reshape(C, tile_rows, block_pixels).transpose(1, 0, 2)

        def row_pass(carry, row_inputs):
            conv_flat, image_flat, mask_row, cotangent_row = row_inputs
            pixel_mask = jnp.broadcast_to(mask_row[None, :, None], (TILE, TILES_DEV, TILE)).reshape(block_pixels)
            pixel_cotangent = jnp.broadcast_to(cotangent_row.T[:, None, :, None], (C, TILE, TILES_DEV, TILE)).reshape(C, block_pixels)
            output, grad_conv, up_term, down_term = block_pass(conv_flat, image_flat, pixel_mask, pixel_cotangent, norm_gain, norm_bias, up_weight, up_bias, down_weight, down_bias, layer_scale)
            embedded = lax.optimization_barrier(jnp.mean(output.reshape(C, TILE, TILES_DEV, TILE), axis=(1, 3))).T
            return ((carry[0] + up_term, carry[1] + down_term), (embedded, grad_conv, pixel_cotangent))
        start = (jnp.zeros((C, HID), jnp.float32), jnp.zeros((C, HID), jnp.float32))
        sums, stacked = lax.scan(row_pass, start, (conv_rows, image_rows, masks, wanted))
        embedded, grad_convs, cotangents = stacked
        grad_image = grad_convs.transpose(1, 0, 2).reshape(C, HEIGHT, WIDTH)
        cotangent_image = cotangents.transpose(1, 0, 2).reshape(C, HEIGHT, WIDTH)
        grad_extended = jnp.pad(grad_image, ((0, 0), (3, 3), (3, 3)))
        input_grad = (cotangent_image + depthwise(grad_extended, depth_kernel, HEIGHT, WIDTH, True)).astype(jnp.bfloat16)
        kernel_cols = []
        for position in range(49):
            row_start = position // 7
            col_start = position % 7
            window = lax.slice(extended, (0, row_start, col_start), (C, row_start + HEIGHT, col_start + WIDTH))
            kernel_cols.append(lax.optimization_barrier(jnp.sum(grad_image.astype(jnp.float32) * window.astype(jnp.float32), axis=(1, 2))))
        kernel_term = jnp.stack(kernel_cols, axis=1)
        return (embedded.reshape(TILES, C), input_grad, sums[0], sums[1], kernel_term)
    results = lax.map(slide_pass, (features, tissue, aggregator_order, tile_cotangent))
    grad_up = lax.optimization_barrier(jnp.sum(results[2], axis=0)) * loss_norm
    grad_down = lax.optimization_barrier(jnp.sum(results[3], axis=0)).T * loss_norm
    grad_kernel = lax.optimization_barrier(jnp.sum(results[4], axis=0)) * loss_norm
    return (results[0], results[1], grad_up, grad_down, grad_kernel)
```

```python
import math

import jax
import jax.numpy as jnp
from jax import lax
from jax.experimental import pallas as pl
from jax.experimental.pallas import tpu as pltpu
from jax.sharding import PartitionSpec as P

TILE = 32
SLOT = 40
PER = 3
ROWS = 4
VMEM = pl.BlockSpec(memory_space=pltpu.VMEM)


def extended_rows(cells, axis):
    channels, height, across = cells.shape
    count = lax.axis_size(axis)
    above = lax.ppermute(cells[:, height - 3 :], axis, [(i, i + 1) for i in range(count - 1)])
    below = lax.ppermute(cells[:, :3], axis, [(i + 1, i) for i in range(count - 1)])
    spare = jnp.zeros((channels, SLOT - height - 6, across), cells.dtype)
    return jnp.concatenate([above, cells, below, spare], axis=1)


def shifted_stack(rows):
    across = rows.shape[1]
    lane = lax.broadcasted_iota(jnp.int32, rows.shape, 1)
    spare = jnp.zeros((across - PER * SLOT, across), jnp.float32)
    pieces = []
    for b in range(7):
        offset = b - 3
        if offset == 0:
            piece = rows
        else:
            piece = pltpu.roll(rows, (-offset) % across, 1)
            inside = lane < across - offset if offset > 0 else lane >= -offset
            piece = jnp.where(inside, piece, 0.0)
        pieces.append(piece)
        if b % PER == PER - 1:
            pieces.append(spare)
    return jnp.concatenate(pieces, axis=0).astype(jnp.bfloat16)


def banded(taps_ref, c, height):
    parts = []
    for g in range(3):
        part = jnp.broadcast_to(taps_ref[g, pl.ds(c, 1), :], (height, 128))
        parts.append(pltpu.roll(part, 0, 1, stride=1, stride_axis=0))
    return jnp.concatenate(parts, axis=1)


def diagonal_sums(cells):
    height, across = cells.shape
    total = cells[:8]
    for start in range(8, height, 8):
        total = total + pltpu.roll(cells[start : start + 8], across - start, 1)
    row = lax.broadcasted_iota(jnp.int32, total.shape, 0)
    for bit in (4, 2, 1):
        total = jnp.where((row // bit) % 2 == 1, pltpu.roll(total, across - bit, 1), total)
    return jnp.sum(total, axis=0, keepdims=True)


def forward_kernel(
    ext_ref, taps_hi, taps_lo, conv_bias, gain_ref, bias_ref, up_ref, up_bias, down_ref,
    down_bias, mask_ref, branch_ref,
    grad_ref, embed_ref, up_out, down_out, held, sums, hidden_sum, slope_gain,
):
    channels, _, across = ext_ref.shape
    height = grad_ref.shape[1]
    hidden_units = up_ref.shape[1]
    depth = 2 * 128 + SLOT

    def conv_channel(c, carry):
        rows = ext_ref[c].astype(jnp.float32)
        stack = shifted_stack(rows)
        hi = banded(taps_hi, c, height)
        lo = banded(taps_lo, c, height)
        left = jnp.concatenate([hi, lo], axis=0).astype(jnp.bfloat16)[:, :depth]
        both = jnp.dot(left, stack, preferred_element_type=jnp.float32)
        held[pl.ds(c, height, stride=channels), :] = both[:height] + both[height:]
        sums[pl.ds(c, 1), :] = jnp.sum(rows, axis=0, keepdims=True) - jnp.sum(
            rows[:3], axis=0, keepdims=True
        ) - jnp.sum(rows[height + 3 :], axis=0, keepdims=True)
        return carry

    lax.fori_loop(0, channels, conv_channel, 0, unroll=4)

    slope_gain[...] = jnp.dot(down_ref[...], branch_ref[...], preferred_element_type=jnp.float32)
    hidden_sum[...] = jnp.zeros_like(hidden_sum)
    up_out[...] = jnp.zeros_like(up_out)

    def pixels(block, carry):
        parts = []
        for r in range(ROWS):
            start = pl.multiple_of((block * ROWS + r) * channels, 8)
            parts.append(held[pl.ds(start, channels), :])
        conv = jnp.concatenate(parts, axis=1) + conv_bias[...]
        average = jnp.mean(conv, axis=0, keepdims=True)
        centered = conv - average
        variance = jnp.mean(centered * centered, axis=0, keepdims=True)
        reciprocal = lax.rsqrt(variance + 1e-06)
        standard = centered * reciprocal
        normed = (standard * gain_ref[...] + bias_ref[...]).astype(jnp.bfloat16)
        act = lax.dot_general(
            up_ref[...], normed, (((0,), (0,)), ((), ())), preferred_element_type=jnp.float32
        )
        act = act + up_bias[...]
        cumulative = 0.5 + 0.5 * lax.erf(act * 0.7071067811865476)
        hidden = (act * cumulative).astype(jnp.bfloat16).astype(jnp.float32)
        total = hidden_sum[...]
        for r in range(ROWS):
            total = total + hidden[:, r * across : (r + 1) * across]
        hidden_sum[...] = total
        density = jnp.exp(-0.5 * act * act) * 0.3989422804014327
        slope = cumulative + act * density
        grad_hidden = jnp.concatenate([slope_gain[...]] * ROWS, axis=1)
        grad_act = (grad_hidden * slope).astype(jnp.bfloat16)
        grad_normed = jnp.dot(up_ref[...], grad_act, preferred_element_type=jnp.float32)
        up_out[...] += lax.dot_general(
            normed, grad_act, (((1,), (1,)), ((), ())), preferred_element_type=jnp.float32
        )
        grad_standard = grad_normed * gain_ref[...]
        first = jnp.mean(grad_standard, axis=0, keepdims=True)
        second = jnp.mean(grad_standard * standard, axis=0, keepdims=True)
        grad_conv = reciprocal * (grad_standard - first - standard * second)
        for r in range(ROWS):
            start = pl.multiple_of((block * ROWS + r) * channels, 8)
            held[pl.ds(start, channels), :] = grad_conv[:, r * across : (r + 1) * across]
        return carry

    lax.fori_loop(0, height // ROWS, pixels, 0)

    total = hidden_sum[...]
    total_hi = total.astype(jnp.bfloat16)
    total_lo = (total - total_hi.astype(jnp.float32)).astype(jnp.bfloat16)
    branch = jnp.zeros((channels, across), jnp.float32)
    down = jnp.zeros((channels, hidden_units), jnp.float32)
    for part in (total_hi, total_lo):
        branch += lax.dot_general(
            down_ref[...], part, (((0,), (0,)), ((), ())), preferred_element_type=jnp.float32
        )
        down += lax.dot_general(
            branch_ref[...], part, (((1,), (1,)), ((), ())), preferred_element_type=jnp.float32
        )
    down_out[...] = down
    embed_ref[...] = sums[...] + mask_ref[...] * (branch + height * down_bias[...])

    def turn(c, carry):
        grad_ref[c] = held[pl.ds(c, height, stride=channels), :].astype(jnp.bfloat16)
        return carry

    lax.fori_loop(0, channels, turn, 0, unroll=8)


def backward_kernel(grad_ref, image_ref, taps_ref, cotangent_ref, out_ref, kernel_ref):
    channels, height, across = image_ref.shape
    depth = 2 * 128 + SLOT

    def channel(c, carry):
        stack = shifted_stack(grad_ref[c].astype(jnp.float32))
        left = banded(taps_ref, c, height).astype(jnp.bfloat16)[:, :depth]
        conv = jnp.dot(left, stack, preferred_element_type=jnp.float32)
        out_ref[c] = (conv + cotangent_ref[pl.ds(c, 1), :]).astype(jnp.bfloat16)
        spare = jnp.zeros((3 * 128 - depth, across), jnp.bfloat16)
        cross = lax.dot_general(
            image_ref[c],
            jnp.concatenate([stack, spare], axis=0),
            (((1,), (1,)), ((), ())),
            preferred_element_type=jnp.float32,
        )
        for g in range(3):
            kernel_ref[g, pl.ds(c, 1), :] = diagonal_sums(cross[:, g * 128 : (g + 1) * 128])
        return carry

    lax.fori_loop(0, channels, channel, 0, unroll=4)


def tap_rows(taps):
    channels = taps.shape[0]
    by_column = jnp.pad(taps.transpose(0, 2, 1), ((0, 0), (0, 2), (0, SLOT - 7)))
    groups = by_column.reshape(channels, 3, PER * SLOT)
    return jnp.pad(groups, ((0, 0), (0, 0), (0, 128 - PER * SLOT))).transpose(1, 0, 2)


def taps_of(rows):
    channels = rows.shape[1]
    groups = rows[:, :, : PER * SLOT].transpose(1, 0, 2).reshape(channels, 9, SLOT)
    return groups[:, :7, :7].transpose(0, 2, 1)


def on_device(
    features,
    depth_kernel,
    depth_bias,
    norm_gain,
    norm_bias,
    up_weight,
    up_bias,
    down_weight,
    down_bias,
    layer_scale,
    tissue,
    aggregator_order,
    tile_cotangent,
):
    image = features[0]
    channels, height, across = image.shape
    tiles_here = across // TILE
    hidden_units = up_weight.shape[1]
    taps = depth_kernel.reshape(channels, 7, 7)
    rows = tap_rows(taps)
    rows_hi = lax.reduce_precision(rows, 8, 7)
    rows_lo = rows - rows_hi
    rows_back = tap_rows(taps[:, ::-1, ::-1])
    gathered = lax.all_gather(tile_cotangent, "rows", axis=1, tiled=True)[0]
    positions = lax.dynamic_slice_in_dim(
        aggregator_order[0], lax.axis_index("rows") * tiles_here, tiles_here
    )
    wanted = jnp.take(gathered, positions, axis=0).astype(jnp.float32)
    cotangent = jnp.repeat(wanted.T, TILE, axis=1)
    mask = jnp.repeat(tissue[0, 0].astype(jnp.float32), TILE)
    scaled_mask = mask[None, :] * layer_scale[:, None]
    grad_branch = (scaled_mask * cotangent).astype(jnp.bfloat16)
    f32 = jnp.float32
    grad_conv, embed, up_term, down_term = pl.pallas_call(
        forward_kernel,
        out_shape=(
            jax.ShapeDtypeStruct((channels, height, across), jnp.bfloat16),
            jax.ShapeDtypeStruct((channels, across), f32),
            jax.ShapeDtypeStruct((channels, hidden_units), f32),
            jax.ShapeDtypeStruct((channels, hidden_units), f32),
        ),
        in_specs=[VMEM] * 12,
        out_specs=(VMEM,) * 4,
        scratch_shapes=[
            pltpu.VMEM((height * channels, across), f32),
            pltpu.VMEM((channels, across), f32),
            pltpu.VMEM((hidden_units, across), f32),
            pltpu.VMEM((hidden_units, across), f32),
        ],
        compiler_params=pltpu.CompilerParams(vmem_limit_bytes=56 * 1024 * 1024),
        name="forward_block",
    )(
        extended_rows(image, "rows"),
        rows_hi,
        rows_lo,
        depth_bias[:, None],
        norm_gain[:, None],
        norm_bias[:, None],
        up_weight,
        up_bias[:, None],
        down_weight,
        down_bias[:, None],
        scaled_mask,
        grad_branch,
    )
    embedding = (
        embed.reshape(channels, tiles_here, TILE).sum(axis=2) / (height * TILE)
    ).T[None]
    input_grad, kernel_rows = pl.pallas_call(
        backward_kernel,
        out_shape=(
            jax.ShapeDtypeStruct((channels, height, across), jnp.bfloat16),
            jax.ShapeDtypeStruct((3, channels, 128), f32),
        ),
        in_specs=[VMEM] * 4,
        out_specs=(VMEM,) * 2,
        compiler_params=pltpu.CompilerParams(vmem_limit_bytes=40 * 1024 * 1024),
        name="backward_conv",
    )(extended_rows(grad_conv, "rows"), image, rows_back, cotangent)
    kernel_term = taps_of(kernel_rows)[:, ::-1, ::-1].reshape(channels, 49)
    loss_norm = 1.0 / math.sqrt(lax.axis_size("slide") * lax.axis_size("rows") * height * across)
    combined = (
        jnp.concatenate(
            [up_term, down_term, kernel_term, jnp.zeros((channels, 15), f32)], axis=1
        )
        * loss_norm
    )
    totals = lax.psum(combined, ("slide", "rows"))
    grad_up = totals[:, :hidden_units]
    grad_down = totals[:, hidden_units : 2 * hidden_units].T
    grad_kernel = totals[:, 2 * hidden_units : 2 * hidden_units + 49]
    return (embedding, input_grad[None], grad_up, grad_down, grad_kernel)


def solution(mesh):
    return jax.shard_map(
        on_device,
        mesh=mesh,
        in_specs=(
            P("slide", None, "rows", None),
            P(),
            P(),
            P(),
            P(),
            P(),
            P(),
            P(),
            P(),
            P(),
            P("slide", "rows", None),
            P("slide", None),
            P("slide", "rows", None),
        ),
        out_specs=(P("slide", "rows", None), P("slide", None, "rows", None), P(), P(), P()),
        check_vma=False,
    )
```

```python
import functools
import math

import jax
import jax.numpy as jnp
from jax import lax
from jax.experimental import pallas as pl
from jax.experimental.pallas import tpu as pltpu
from jax.sharding import PartitionSpec as P

TILE = 32
SLOT = 40
PER = 3
ROWS = 4
MESH = pl.DeviceIdType.MESH
VMEM = pl.BlockSpec(memory_space=pltpu.VMEM)


def greet(peers):
    barrier = pltpu.get_barrier_semaphore()
    for peer in peers:
        pl.semaphore_signal(barrier, inc=1, device_id=peer, device_id_type=MESH)
    pl.semaphore_wait(barrier, len(peers))


def remote(source, target, send, receive, peer):
    copy = pltpu.make_async_remote_copy(
        src_ref=source,
        dst_ref=target,
        send_sem=send,
        recv_sem=receive,
        device_id=peer,
        device_id_type=MESH,
    )
    copy.start()
    return copy


def halo_kernel(count, gathers, head_ref, tail_ref, *refs):
    if gathers:
        block_ref, above_ref, below_ref, all_ref, edge_send, edge_recv, send, recv, own = refs
    else:
        above_ref, below_ref, edge_send, edge_recv = refs
    slide, me = lax.axis_index("slide"), lax.axis_index("rows")
    peers = [(slide, lax.rem(me + k, count)) for k in range(1, count)]
    up, down = peers[-1], peers[0]
    greet(peers if gathers else [up, down])
    copies = []
    if gathers:
        for k in range(1, count):
            copies.append(
                remote(block_ref, all_ref.at[me], send.at[k], recv.at[k], peers[k - 1])
            )
    copies.append(remote(tail_ref, above_ref, edge_send.at[0], edge_recv.at[0], down))
    copies.append(remote(head_ref, below_ref, edge_send.at[1], edge_recv.at[1], up))
    if gathers:
        mine = pltpu.make_async_copy(block_ref, all_ref.at[me], own)
        mine.start()
        mine.wait()
    for copy in copies:
        copy.wait()


def halo(cells, count, channel_id, block=None):
    channels, height, across = cells.shape
    gathers = block is not None
    operands = [cells[:, :3], cells[:, height - 3 :]]
    edge = jax.ShapeDtypeStruct((channels, 3, across), cells.dtype)
    shapes = [edge, edge]
    scratch = [pltpu.SemaphoreType.DMA((2,)), pltpu.SemaphoreType.DMA((2,))]
    if gathers:
        operands.append(block)
        shapes.append(jax.ShapeDtypeStruct((count,) + block.shape, block.dtype))
        scratch += [
            pltpu.SemaphoreType.DMA((count,)),
            pltpu.SemaphoreType.DMA((count,)),
            pltpu.SemaphoreType.DMA,
        ]
    above, below, *rest = pl.pallas_call(
        functools.partial(halo_kernel, count, gathers),
        out_shape=tuple(shapes),
        in_specs=[VMEM] * len(operands),
        out_specs=(VMEM,) * len(shapes),
        scratch_shapes=scratch,
        compiler_params=pltpu.CompilerParams(collective_id=channel_id, has_side_effects=True),
        name="halo",
    )(*operands)
    me = lax.axis_index("rows")
    above = jnp.where(me > 0, above, jnp.zeros_like(above))
    below = jnp.where(me < count - 1, below, jnp.zeros_like(below))
    spare = jnp.zeros((channels, SLOT - height - 6, across), cells.dtype)
    return jnp.concatenate([above, cells, below, spare], axis=1), *rest


def sum_kernel(slides, count, part_ref, out_ref, near, half, far, send, recv):
    slide, me = lax.axis_index("slide"), lax.axis_index("rows")
    across = [(lax.rem(slide + k, slides), me) for k in range(1, slides)]
    along = [(slide, lax.rem(me + k, count)) for k in range(1, count)]
    greet(across + along)
    first = [
        remote(part_ref.at[peer[0]], near.at[k], send.at[0, k], recv.at[0, k], peer)
        for k, peer in enumerate(across)
    ]
    for copy in first:
        copy.wait()
    total = part_ref[slide].astype(jnp.float32)
    for k in range(slides - 1):
        total = total + near[k].astype(jnp.float32)
    half[...] = total.astype(jnp.bfloat16)
    second = [
        remote(half.at[peer[1]], far.at[k], send.at[1, k], recv.at[1, k], peer)
        for k, peer in enumerate(along)
    ]
    for copy in second:
        copy.wait()
    total = half[me].astype(jnp.float32)
    for k in range(count - 1):
        total = total + far[k].astype(jnp.float32)
    out_ref[slide, me] = total.astype(jnp.bfloat16)
    third = [
        remote(out_ref.at[slide, me], out_ref.at[slide, me], send.at[2, k], recv.at[2, k], peer)
        for k, peer in enumerate(along)
    ]
    for copy in third:
        copy.wait()
    fourth = [
        remote(out_ref.at[slide], out_ref.at[slide], send.at[3, k], recv.at[3, k], peer)
        for k, peer in enumerate(across)
    ]
    for copy in fourth:
        copy.wait()


def sum_everywhere(rows, slides, count):
    length, across = rows.shape
    share = 16 * pl.cdiv(length, 16 * slides * count)
    padded = jnp.pad(rows, ((0, slides * count * share - length), (0, 0))).astype(jnp.bfloat16)
    shape = (slides, count, share, across)
    totals = pl.pallas_call(
        functools.partial(sum_kernel, slides, count),
        out_shape=jax.ShapeDtypeStruct(shape, jnp.bfloat16),
        in_specs=[VMEM],
        out_specs=VMEM,
        scratch_shapes=[
            pltpu.VMEM((slides - 1,) + shape[1:], jnp.bfloat16),
            pltpu.VMEM(shape[1:], jnp.bfloat16),
            pltpu.VMEM((count - 1,) + shape[2:], jnp.bfloat16),
            pltpu.SemaphoreType.DMA((4, max(slides, count) - 1)),
            pltpu.SemaphoreType.DMA((4, max(slides, count) - 1)),
        ],
        compiler_params=pltpu.CompilerParams(collective_id=2, has_side_effects=True),
        name="sum_everywhere",
    )(padded.reshape(shape))
    return totals.reshape(-1, across)[:length].astype(jnp.float32)


def shifted_stack(rows):
    across = rows.shape[1]
    lane = lax.broadcasted_iota(jnp.int32, rows.shape, 1)
    spare = jnp.zeros((across - PER * SLOT, across), jnp.float32)
    pieces = []
    for b in range(7):
        offset = b - 3
        if offset == 0:
            piece = rows
        else:
            piece = pltpu.roll(rows, (-offset) % across, 1)
            inside = lane < across - offset if offset > 0 else lane >= -offset
            piece = jnp.where(inside, piece, 0.0)
        pieces.append(piece)
        if b % PER == PER - 1:
            pieces.append(spare)
    return jnp.concatenate(pieces, axis=0).astype(jnp.bfloat16)


def banded(taps_ref, c, height):
    parts = []
    for g in range(3):
        part = jnp.broadcast_to(taps_ref[g, pl.ds(c, 1), :], (height, 128))
        parts.append(pltpu.roll(part, 0, 1, stride=1, stride_axis=0))
    return jnp.concatenate(parts, axis=1)


def diagonal_sums(cells):
    height, across = cells.shape
    total = cells[:8]
    for start in range(8, height, 8):
        total = total + pltpu.roll(cells[start : start + 8], across - start, 1)
    row = lax.broadcasted_iota(jnp.int32, total.shape, 0)
    for bit in (4, 2, 1):
        total = jnp.where((row // bit) % 2 == 1, pltpu.roll(total, across - bit, 1), total)
    return jnp.sum(total, axis=0, keepdims=True)


def forward_kernel(
    ext_ref, taps_hi, taps_lo, conv_bias, gain_ref, bias_ref, up_ref, up_bias, down_ref,
    down_bias, mask_ref, branch_ref,
    grad_ref, embed_ref, up_out, down_out, held, sums, hidden_sum, slope_gain,
):
    channels, _, across = ext_ref.shape
    height = grad_ref.shape[1]
    hidden_units = up_ref.shape[1]
    depth = 2 * 128 + SLOT

    def conv_channel(c, carry):
        rows = ext_ref[c].astype(jnp.float32)
        stack = shifted_stack(rows)
        hi = banded(taps_hi, c, height)
        lo = banded(taps_lo, c, height)
        left = jnp.concatenate([hi, lo], axis=0).astype(jnp.bfloat16)[:, :depth]
        both = jnp.dot(left, stack, preferred_element_type=jnp.float32)
        held[pl.ds(c, height, stride=channels), :] = both[:height] + both[height:]
        sums[pl.ds(c, 1), :] = jnp.sum(rows, axis=0, keepdims=True) - jnp.sum(
            rows[:3], axis=0, keepdims=True
        ) - jnp.sum(rows[height + 3 :], axis=0, keepdims=True)
        return carry

    lax.fori_loop(0, channels, conv_channel, 0, unroll=4)

    slope_gain[...] = jnp.dot(down_ref[...], branch_ref[...], preferred_element_type=jnp.float32)
    hidden_sum[...] = jnp.zeros_like(hidden_sum)
    up_out[...] = jnp.zeros_like(up_out)

    def pixels(block, carry):
        parts = []
        for r in range(ROWS):
            start = pl.multiple_of((block * ROWS + r) * channels, 8)
            parts.append(held[pl.ds(start, channels), :])
        conv = jnp.concatenate(parts, axis=1) + conv_bias[...]
        average = jnp.mean(conv, axis=0, keepdims=True)
        centered = conv - average
        variance = jnp.mean(centered * centered, axis=0, keepdims=True)
        reciprocal = lax.rsqrt(variance + 1e-06)
        standard = centered * reciprocal
        normed = (standard * gain_ref[...] + bias_ref[...]).astype(jnp.bfloat16)
        act = lax.dot_general(
            up_ref[...], normed, (((0,), (0,)), ((), ())), preferred_element_type=jnp.float32
        )
        act = act + up_bias[...]
        cumulative = 0.5 + 0.5 * lax.erf(act * 0.7071067811865476)
        hidden = (act * cumulative).astype(jnp.bfloat16).astype(jnp.float32)
        total = hidden_sum[...]
        for r in range(ROWS):
            total = total + hidden[:, r * across : (r + 1) * across]
        hidden_sum[...] = total
        density = jnp.exp(-0.5 * act * act) * 0.3989422804014327
        slope = cumulative + act * density
        grad_hidden = jnp.concatenate([slope_gain[...]] * ROWS, axis=1)
        grad_act = (grad_hidden * slope).astype(jnp.bfloat16)
        grad_normed = jnp.dot(up_ref[...], grad_act, preferred_element_type=jnp.float32)
        up_out[...] += lax.dot_general(
            normed, grad_act, (((1,), (1,)), ((), ())), preferred_element_type=jnp.float32
        )
        grad_standard = grad_normed * gain_ref[...]
        first = jnp.mean(grad_standard, axis=0, keepdims=True)
        second = jnp.mean(grad_standard * standard, axis=0, keepdims=True)
        grad_conv = reciprocal * (grad_standard - first - standard * second)
        for r in range(ROWS):
            start = pl.multiple_of((block * ROWS + r) * channels, 8)
            held[pl.ds(start, channels), :] = grad_conv[:, r * across : (r + 1) * across]
        return carry

    lax.fori_loop(0, height // ROWS, pixels, 0)

    total = hidden_sum[...]
    total_hi = total.astype(jnp.bfloat16)
    total_lo = (total - total_hi.astype(jnp.float32)).astype(jnp.bfloat16)
    branch = jnp.zeros((channels, across), jnp.float32)
    down = jnp.zeros((channels, hidden_units), jnp.float32)
    for part in (total_hi, total_lo):
        branch += lax.dot_general(
            down_ref[...], part, (((0,), (0,)), ((), ())), preferred_element_type=jnp.float32
        )
        down += lax.dot_general(
            branch_ref[...], part, (((1,), (1,)), ((), ())), preferred_element_type=jnp.float32
        )
    down_out[...] = down
    embed_ref[...] = sums[...] + mask_ref[...] * (branch + height * down_bias[...])

    def turn(c, carry):
        grad_ref[c] = held[pl.ds(c, height, stride=channels), :].astype(jnp.bfloat16)
        return carry

    lax.fori_loop(0, channels, turn, 0, unroll=8)


def backward_kernel(grad_ref, image_ref, taps_ref, cotangent_ref, out_ref, kernel_ref):
    channels, height, across = image_ref.shape
    depth = 2 * 128 + SLOT

    def channel(c, carry):
        stack = shifted_stack(grad_ref[c].astype(jnp.float32))
        left = banded(taps_ref, c, height).astype(jnp.bfloat16)[:, :depth]
        conv = jnp.dot(left, stack, preferred_element_type=jnp.float32)
        out_ref[c] = (conv + cotangent_ref[pl.ds(c, 1), :]).astype(jnp.bfloat16)
        spare = jnp.zeros((3 * 128 - depth, across), jnp.bfloat16)
        cross = lax.dot_general(
            image_ref[c],
            jnp.concatenate([stack, spare], axis=0),
            (((1,), (1,)), ((), ())),
            preferred_element_type=jnp.float32,
        )
        for g in range(3):
            kernel_ref[g, pl.ds(c, 1), :] = diagonal_sums(cross[:, g * 128 : (g + 1) * 128])
        return carry

    lax.fori_loop(0, channels, channel, 0, unroll=4)


def tap_rows(taps):
    channels = taps.shape[0]
    by_column = jnp.pad(taps.transpose(0, 2, 1), ((0, 0), (0, 2), (0, SLOT - 7)))
    groups = by_column.reshape(channels, 3, PER * SLOT)
    return jnp.pad(groups, ((0, 0), (0, 0), (0, 128 - PER * SLOT))).transpose(1, 0, 2)


def taps_of(rows):
    channels = rows.shape[1]
    groups = rows[:, :, : PER * SLOT].transpose(1, 0, 2).reshape(channels, 9, SLOT)
    return groups[:, :7, :7].transpose(0, 2, 1)


def on_device(
    features,
    depth_kernel,
    depth_bias,
    norm_gain,
    norm_bias,
    up_weight,
    up_bias,
    down_weight,
    down_bias,
    layer_scale,
    tissue,
    aggregator_order,
    tile_cotangent,
):
    image = features[0]
    channels, height, across = image.shape
    tiles_here = across // TILE
    hidden_units = up_weight.shape[1]
    taps = depth_kernel.reshape(channels, 7, 7)
    rows = tap_rows(taps)
    rows_hi = lax.reduce_precision(rows, 8, 7)
    rows_lo = rows - rows_hi
    rows_back = tap_rows(taps[:, ::-1, ::-1])
    slides, count = lax.axis_size("slide"), lax.axis_size("rows")
    extended, gathered = halo(image, count, 0, tile_cotangent[0])
    gathered = gathered.reshape(count * tiles_here, channels)
    positions = lax.dynamic_slice_in_dim(
        aggregator_order[0], lax.axis_index("rows") * tiles_here, tiles_here
    )
    wanted = jnp.take(gathered, positions, axis=0).astype(jnp.float32)
    cotangent = jnp.repeat(wanted.T, TILE, axis=1)
    mask = jnp.repeat(tissue[0, 0].astype(jnp.float32), TILE)
    scaled_mask = mask[None, :] * layer_scale[:, None]
    grad_branch = (scaled_mask * cotangent).astype(jnp.bfloat16)
    f32 = jnp.float32
    grad_conv, embed, up_term, down_term = pl.pallas_call(
        forward_kernel,
        out_shape=(
            jax.ShapeDtypeStruct((channels, height, across), jnp.bfloat16),
            jax.ShapeDtypeStruct((channels, across), f32),
            jax.ShapeDtypeStruct((channels, hidden_units), f32),
            jax.ShapeDtypeStruct((channels, hidden_units), f32),
        ),
        in_specs=[VMEM] * 12,
        out_specs=(VMEM,) * 4,
        scratch_shapes=[
            pltpu.VMEM((height * channels, across), f32),
            pltpu.VMEM((channels, across), f32),
            pltpu.VMEM((hidden_units, across), f32),
            pltpu.VMEM((hidden_units, across), f32),
        ],
        compiler_params=pltpu.CompilerParams(vmem_limit_bytes=56 * 1024 * 1024),
        name="forward_block",
    )(
        extended,
        rows_hi,
        rows_lo,
        depth_bias[:, None],
        norm_gain[:, None],
        norm_bias[:, None],
        up_weight,
        up_bias[:, None],
        down_weight,
        down_bias[:, None],
        scaled_mask,
        grad_branch,
    )
    embedding = (
        embed.reshape(channels, tiles_here, TILE).sum(axis=2) / (height * TILE)
    ).T[None]
    (grad_extended,) = halo(grad_conv, count, 1)
    input_grad, kernel_rows = pl.pallas_call(
        backward_kernel,
        out_shape=(
            jax.ShapeDtypeStruct((channels, height, across), jnp.bfloat16),
            jax.ShapeDtypeStruct((3, channels, 128), f32),
        ),
        in_specs=[VMEM] * 4,
        out_specs=(VMEM,) * 2,
        compiler_params=pltpu.CompilerParams(vmem_limit_bytes=40 * 1024 * 1024),
        name="backward_conv",
    )(grad_extended, image, rows_back, cotangent)
    kernel_term = taps_of(kernel_rows)[:, ::-1, ::-1].reshape(channels, 49)
    loss_norm = 1.0 / math.sqrt(slides * count * height * across)
    tap_lanes = kernel_term.shape[1]
    wide = jnp.pad(kernel_term, ((0, 0), (0, across - tap_lanes)))
    blocks = hidden_units // across
    combined = jnp.concatenate(
        [
            up_term.reshape(channels, blocks, across).transpose(1, 0, 2),
            down_term.reshape(channels, blocks, across).transpose(1, 0, 2),
            wide[None],
        ],
        axis=0,
    )
    totals = sum_everywhere((combined * loss_norm).reshape(-1, across), slides, count)
    totals = totals.reshape(2 * blocks + 1, channels, across)
    grad_up = totals[:blocks].transpose(1, 0, 2).reshape(channels, hidden_units)
    grad_down = totals[blocks : 2 * blocks].transpose(0, 2, 1).reshape(hidden_units, channels)
    grad_kernel = totals[2 * blocks, :, :tap_lanes]
    return (embedding, input_grad[None], grad_up, grad_down, grad_kernel)


def solution(mesh):
    return jax.shard_map(
        on_device,
        mesh=mesh,
        in_specs=(
            P("slide", None, "rows", None),
            P(),
            P(),
            P(),
            P(),
            P(),
            P(),
            P(),
            P(),
            P(),
            P("slide", "rows", None),
            P("slide", None),
            P("slide", "rows", None),
        ),
        out_specs=(P("slide", "rows", None), P("slide", None, "rows", None), P(), P(), P()),
        check_vma=False,
    )
```

```python
import functools
import math

import jax
import jax.numpy as jnp
from jax import lax
from jax.experimental import pallas as pl
from jax.experimental.pallas import tpu as pltpu
from jax.sharding import PartitionSpec as P

TILE = 32
SLOT = 40
PER = 3
ROWS = 4
MESH = pl.DeviceIdType.MESH
VMEM = pl.BlockSpec(memory_space=pltpu.VMEM)


def greet(peers):
    barrier = pltpu.get_barrier_semaphore()
    for peer in peers:
        pl.semaphore_signal(barrier, inc=1, device_id=peer, device_id_type=MESH)
    pl.semaphore_wait(barrier, len(peers))


def remote(source, target, send, receive, peer):
    copy = pltpu.make_async_remote_copy(
        src_ref=source,
        dst_ref=target,
        send_sem=send,
        recv_sem=receive,
        device_id=peer,
        device_id_type=MESH,
    )
    copy.start()
    return copy


def halo_kernel(count, gathers, head_ref, tail_ref, *refs):
    if gathers:
        block_ref, above_ref, below_ref, all_ref, edge_send, edge_recv, send, recv, own = refs
    else:
        above_ref, below_ref, edge_send, edge_recv = refs
    slide, me = lax.axis_index("slide"), lax.axis_index("rows")
    peers = [(slide, lax.rem(me + k, count)) for k in range(1, count)]
    up, down = peers[-1], peers[0]
    greet(peers if gathers else [up, down])
    copies = []
    if gathers:
        for k in range(1, count):
            copies.append(
                remote(block_ref, all_ref.at[me], send.at[k], recv.at[k], peers[k - 1])
            )
    copies.append(remote(tail_ref, above_ref, edge_send.at[0], edge_recv.at[0], down))
    copies.append(remote(head_ref, below_ref, edge_send.at[1], edge_recv.at[1], up))
    if gathers:
        mine = pltpu.make_async_copy(block_ref, all_ref.at[me], own)
        mine.start()
        mine.wait()
    for copy in copies:
        copy.wait()


def halo(cells, count, channel_id, block=None):
    channels, height, across = cells.shape
    gathers = block is not None
    turned = cells.transpose(1, 0, 2)
    operands = [turned[:3], turned[height - 3 :]]
    edge = jax.ShapeDtypeStruct((3, channels, across), cells.dtype)
    shapes = [edge, edge]
    scratch = [pltpu.SemaphoreType.DMA((2,)), pltpu.SemaphoreType.DMA((2,))]
    if gathers:
        operands.append(block)
        shapes.append(jax.ShapeDtypeStruct((count,) + block.shape, block.dtype))
        scratch += [
            pltpu.SemaphoreType.DMA((count,)),
            pltpu.SemaphoreType.DMA((count,)),
            pltpu.SemaphoreType.DMA,
        ]
    above, below, *rest = pl.pallas_call(
        functools.partial(halo_kernel, count, gathers),
        out_shape=tuple(shapes),
        in_specs=[VMEM] * len(operands),
        out_specs=(VMEM,) * len(shapes),
        scratch_shapes=scratch,
        compiler_params=pltpu.CompilerParams(collective_id=channel_id, has_side_effects=True),
        name="halo",
    )(*operands)
    me = lax.axis_index("rows")
    above = jnp.where(me > 0, above, jnp.zeros_like(above))
    below = jnp.where(me < count - 1, below, jnp.zeros_like(below))
    spare = jnp.zeros((channels, SLOT - height - 6, across), cells.dtype)
    above, below = above.transpose(1, 0, 2), below.transpose(1, 0, 2)
    return jnp.concatenate([above, cells, below, spare], axis=1), *rest


def sum_kernel(slides, count, part_ref, out_ref, near, half, far, send, recv):
    slide, me = lax.axis_index("slide"), lax.axis_index("rows")
    across = [(lax.rem(slide + k, slides), me) for k in range(1, slides)]
    along = [(slide, lax.rem(me + k, count)) for k in range(1, count)]
    greet(across + along)
    first = [
        remote(part_ref.at[peer[0]], near.at[k], send.at[0, k], recv.at[0, k], peer)
        for k, peer in enumerate(across)
    ]
    for copy in first:
        copy.wait()
    total = part_ref[slide].astype(jnp.float32)
    for k in range(slides - 1):
        total = total + near[k].astype(jnp.float32)
    half[...] = total.astype(jnp.bfloat16)
    second = [
        remote(half.at[peer[1]], far.at[k], send.at[1, k], recv.at[1, k], peer)
        for k, peer in enumerate(along)
    ]
    for copy in second:
        copy.wait()
    total = half[me].astype(jnp.float32)
    for k in range(count - 1):
        total = total + far[k].astype(jnp.float32)
    out_ref[slide, me] = total.astype(jnp.bfloat16)
    third = [
        remote(out_ref.at[slide, me], out_ref.at[slide, me], send.at[2, k], recv.at[2, k], peer)
        for k, peer in enumerate(along)
    ]
    for copy in third:
        copy.wait()
    fourth = [
        remote(out_ref.at[slide], out_ref.at[slide], send.at[3, k], recv.at[3, k], peer)
        for k, peer in enumerate(across)
    ]
    for copy in fourth:
        copy.wait()


def sum_everywhere(rows, slides, count):
    length, across = rows.shape
    share = 16 * pl.cdiv(length, 16 * slides * count)
    padded = jnp.pad(rows, ((0, slides * count * share - length), (0, 0))).astype(jnp.bfloat16)
    shape = (slides, count, share, across)
    totals = pl.pallas_call(
        functools.partial(sum_kernel, slides, count),
        out_shape=jax.ShapeDtypeStruct(shape, jnp.bfloat16),
        in_specs=[VMEM],
        out_specs=VMEM,
        scratch_shapes=[
            pltpu.VMEM((slides - 1,) + shape[1:], jnp.bfloat16),
            pltpu.VMEM(shape[1:], jnp.bfloat16),
            pltpu.VMEM((count - 1,) + shape[2:], jnp.bfloat16),
            pltpu.SemaphoreType.DMA((4, max(slides, count) - 1)),
            pltpu.SemaphoreType.DMA((4, max(slides, count) - 1)),
        ],
        compiler_params=pltpu.CompilerParams(collective_id=2, has_side_effects=True),
        name="sum_everywhere",
    )(padded.reshape(shape))
    return totals.reshape(-1, across)[:length].astype(jnp.float32)


def shifted_stack(rows):
    across = rows.shape[1]
    lane = lax.broadcasted_iota(jnp.int32, rows.shape, 1)
    spare = jnp.zeros((across - PER * SLOT, across), jnp.float32)
    pieces = []
    for b in range(7):
        offset = b - 3
        if offset == 0:
            piece = rows
        else:
            piece = pltpu.roll(rows, (-offset) % across, 1)
            inside = lane < across - offset if offset > 0 else lane >= -offset
            piece = jnp.where(inside, piece, 0.0)
        pieces.append(piece)
        if b % PER == PER - 1:
            pieces.append(spare)
    return jnp.concatenate(pieces, axis=0).astype(jnp.bfloat16)


def banded(taps_ref, c, height):
    parts = []
    for g in range(3):
        part = jnp.broadcast_to(taps_ref[g, pl.ds(c, 1), :], (height, 128))
        parts.append(pltpu.roll(part, 0, 1, stride=1, stride_axis=0))
    return jnp.concatenate(parts, axis=1)


def diagonal_sums(cells):
    height, across = cells.shape
    total = cells[:8]
    for start in range(8, height, 8):
        total = total + pltpu.roll(cells[start : start + 8], across - start, 1)
    row = lax.broadcasted_iota(jnp.int32, total.shape, 0)
    for bit in (4, 2, 1):
        total = jnp.where((row // bit) % 2 == 1, pltpu.roll(total, across - bit, 1), total)
    return jnp.sum(total, axis=0, keepdims=True)


def forward_kernel(
    ext_ref, taps_hi, taps_lo, channel_ref, up_ref, up_bias, down_ref, mask_ref, branch_ref,
    grad_ref, embed_ref, up_out, down_out, held, sums, hidden_sum, slope_gain,
):
    conv_bias, gain_ref, bias_ref, down_bias = [channel_ref.at[i] for i in range(4)]
    channels, _, across = ext_ref.shape
    height = grad_ref.shape[1]
    hidden_units = up_ref.shape[1]
    depth = 2 * 128 + SLOT

    def conv_channel(c, carry):
        rows = ext_ref[c].astype(jnp.float32)
        stack = shifted_stack(rows)
        hi = banded(taps_hi, c, height)
        lo = banded(taps_lo, c, height)
        left = jnp.concatenate([hi, lo], axis=0).astype(jnp.bfloat16)[:, :depth]
        both = jnp.dot(left, stack, preferred_element_type=jnp.float32)
        held[pl.ds(c, height, stride=channels), :] = both[:height] + both[height:]
        sums[pl.ds(c, 1), :] = jnp.sum(rows, axis=0, keepdims=True) - jnp.sum(
            rows[:3], axis=0, keepdims=True
        ) - jnp.sum(rows[height + 3 :], axis=0, keepdims=True)
        return carry

    lax.fori_loop(0, channels, conv_channel, 0, unroll=8)

    slope_gain[...] = jnp.dot(down_ref[...], branch_ref[...], preferred_element_type=jnp.float32)
    hidden_sum[...] = jnp.zeros_like(hidden_sum)
    up_out[...] = jnp.zeros_like(up_out)

    def pixels(block, carry):
        parts = []
        for r in range(ROWS):
            start = pl.multiple_of((block * ROWS + r) * channels, 8)
            parts.append(held[pl.ds(start, channels), :])
        conv = jnp.concatenate(parts, axis=1) + conv_bias[...]
        average = jnp.mean(conv, axis=0, keepdims=True)
        centered = conv - average
        variance = jnp.mean(centered * centered, axis=0, keepdims=True)
        reciprocal = lax.rsqrt(variance + 1e-06)
        standard = centered * reciprocal
        normed = (standard * gain_ref[...] + bias_ref[...]).astype(jnp.bfloat16)
        act = lax.dot_general(
            up_ref[...], normed, (((0,), (0,)), ((), ())), preferred_element_type=jnp.float32
        )
        act = act + up_bias[...]
        cumulative = 0.5 + 0.5 * lax.erf(act * 0.7071067811865476)
        hidden = (act * cumulative).astype(jnp.bfloat16).astype(jnp.float32)
        total = hidden_sum[...]
        for r in range(ROWS):
            total = total + hidden[:, r * across : (r + 1) * across]
        hidden_sum[...] = total
        density = jnp.exp(-0.5 * act * act) * 0.3989422804014327
        slope = cumulative + act * density
        grad_hidden = jnp.concatenate([slope_gain[...]] * ROWS, axis=1)
        grad_act = (grad_hidden * slope).astype(jnp.bfloat16)
        grad_normed = jnp.dot(up_ref[...], grad_act, preferred_element_type=jnp.float32)
        up_out[...] += lax.dot_general(
            normed, grad_act, (((1,), (1,)), ((), ())), preferred_element_type=jnp.float32
        )
        grad_standard = grad_normed * gain_ref[...]
        first = jnp.mean(grad_standard, axis=0, keepdims=True)
        second = jnp.mean(grad_standard * standard, axis=0, keepdims=True)
        grad_conv = reciprocal * (grad_standard - first - standard * second)
        for r in range(ROWS):
            start = pl.multiple_of((block * ROWS + r) * channels, 8)
            held[pl.ds(start, channels), :] = grad_conv[:, r * across : (r + 1) * across]
        return carry

    lax.fori_loop(0, height // ROWS, pixels, 0)

    total = hidden_sum[...]
    total_hi = total.astype(jnp.bfloat16)
    total_lo = (total - total_hi.astype(jnp.float32)).astype(jnp.bfloat16)
    branch = jnp.zeros((channels, across), jnp.float32)
    down = jnp.zeros((channels, hidden_units), jnp.float32)
    for part in (total_hi, total_lo):
        branch += lax.dot_general(
            down_ref[...], part, (((0,), (0,)), ((), ())), preferred_element_type=jnp.float32
        )
        down += lax.dot_general(
            branch_ref[...], part, (((1,), (1,)), ((), ())), preferred_element_type=jnp.float32
        )
    down_out[...] = down
    embed_ref[...] = sums[...] + mask_ref[...] * (branch + height * down_bias[...])

    def turn(c, carry):
        grad_ref[c] = held[pl.ds(c, height, stride=channels), :].astype(jnp.bfloat16)
        return carry

    lax.fori_loop(0, channels, turn, 0, unroll=8)


def backward_kernel(grad_ref, image_ref, taps_ref, cotangent_ref, out_ref, kernel_ref):
    channels, height, across = image_ref.shape
    depth = 2 * 128 + SLOT

    def channel(c, carry):
        stack = shifted_stack(grad_ref[c].astype(jnp.float32))
        left = banded(taps_ref, c, height).astype(jnp.bfloat16)[:, :depth]
        conv = jnp.dot(left, stack, preferred_element_type=jnp.float32)
        out_ref[c] = (conv + cotangent_ref[pl.ds(c, 1), :]).astype(jnp.bfloat16)
        spare = jnp.zeros((3 * 128 - depth, across), jnp.bfloat16)
        cross = lax.dot_general(
            image_ref[c],
            jnp.concatenate([stack, spare], axis=0),
            (((1,), (1,)), ((), ())),
            preferred_element_type=jnp.float32,
        )
        for g in range(3):
            kernel_ref[g, pl.ds(c, 1), :] = diagonal_sums(cross[:, g * 128 : (g + 1) * 128])
        return carry

    lax.fori_loop(0, channels, channel, 0, unroll=8)


def tap_rows(taps):
    channels = taps.shape[0]
    by_column = jnp.pad(taps.transpose(0, 2, 1), ((0, 0), (0, 2), (0, SLOT - 7)))
    groups = by_column.reshape(channels, 3, PER * SLOT)
    return jnp.pad(groups, ((0, 0), (0, 0), (0, 128 - PER * SLOT))).transpose(1, 0, 2)


def taps_of(rows):
    channels = rows.shape[1]
    groups = rows[:, :, : PER * SLOT].transpose(1, 0, 2).reshape(channels, 9, SLOT)
    return groups[:, :7, :7].transpose(0, 2, 1)


def on_device(
    features,
    depth_kernel,
    depth_bias,
    norm_gain,
    norm_bias,
    up_weight,
    up_bias,
    down_weight,
    down_bias,
    layer_scale,
    tissue,
    aggregator_order,
    tile_cotangent,
):
    image = features[0]
    channels, height, across = image.shape
    tiles_here = across // TILE
    hidden_units = up_weight.shape[1]
    taps = depth_kernel.reshape(channels, 7, 7)
    rows = tap_rows(taps)
    rows_hi = lax.reduce_precision(rows, 8, 7)
    rows_lo = rows - rows_hi
    rows_back = tap_rows(taps[:, ::-1, ::-1])
    slides, count = lax.axis_size("slide"), lax.axis_size("rows")
    extended, gathered = halo(image, count, 0, tile_cotangent[0])
    gathered = gathered.reshape(count * tiles_here, channels)
    positions = lax.dynamic_slice_in_dim(
        aggregator_order[0], lax.axis_index("rows") * tiles_here, tiles_here
    )
    wanted = jnp.take(gathered, positions, axis=0).astype(jnp.float32)
    cotangent = jnp.repeat(wanted.T, TILE, axis=1)
    mask = jnp.repeat(tissue[0, 0].astype(jnp.float32), TILE)
    scaled_mask = mask[None, :] * layer_scale[:, None]
    grad_branch = (scaled_mask * cotangent).astype(jnp.bfloat16)
    f32 = jnp.float32
    grad_conv, embed, up_term, down_term = pl.pallas_call(
        forward_kernel,
        out_shape=(
            jax.ShapeDtypeStruct((channels, height, across), jnp.bfloat16),
            jax.ShapeDtypeStruct((channels, across), f32),
            jax.ShapeDtypeStruct((channels, hidden_units), f32),
            jax.ShapeDtypeStruct((channels, hidden_units), f32),
        ),
        in_specs=[VMEM] * 9,
        out_specs=(VMEM,) * 4,
        scratch_shapes=[
            pltpu.VMEM((height * channels, across), f32),
            pltpu.VMEM((channels, across), f32),
            pltpu.VMEM((hidden_units, across), f32),
            pltpu.VMEM((hidden_units, across), f32),
        ],
        compiler_params=pltpu.CompilerParams(vmem_limit_bytes=56 * 1024 * 1024),
        name="forward_block",
    )(
        extended,
        rows_hi,
        rows_lo,
        jnp.stack([depth_bias, norm_gain, norm_bias, down_bias])[:, :, None],
        up_weight,
        up_bias[:, None],
        down_weight,
        scaled_mask,
        grad_branch,
    )
    embedding = (
        embed.reshape(channels, tiles_here, TILE).sum(axis=2) / (height * TILE)
    ).T[None]
    (grad_extended,) = halo(grad_conv, count, 1)
    input_grad, kernel_rows = pl.pallas_call(
        backward_kernel,
        out_shape=(
            jax.ShapeDtypeStruct((channels, height, across), jnp.bfloat16),
            jax.ShapeDtypeStruct((3, channels, 128), f32),
        ),
        in_specs=[VMEM] * 4,
        out_specs=(VMEM,) * 2,
        compiler_params=pltpu.CompilerParams(vmem_limit_bytes=40 * 1024 * 1024),
        name="backward_conv",
    )(grad_extended, image, rows_back, cotangent)
    kernel_term = taps_of(kernel_rows)[:, ::-1, ::-1].reshape(channels, 49)
    loss_norm = 1.0 / math.sqrt(slides * count * height * across)
    tap_lanes = kernel_term.shape[1]
    wide = jnp.pad(kernel_term, ((0, 0), (0, across - tap_lanes)))
    blocks = hidden_units // across
    combined = jnp.concatenate(
        [
            up_term.reshape(channels, blocks, across).transpose(1, 0, 2),
            down_term.reshape(channels, blocks, across).transpose(1, 0, 2),
            wide[None],
        ],
        axis=0,
    )
    totals = sum_everywhere((combined * loss_norm).reshape(-1, across), slides, count)
    totals = totals.reshape(2 * blocks + 1, channels, across)
    grad_up = totals[:blocks].transpose(1, 0, 2).reshape(channels, hidden_units)
    grad_down = totals[blocks : 2 * blocks].transpose(0, 2, 1).reshape(hidden_units, channels)
    grad_kernel = totals[2 * blocks, :, :tap_lanes]
    return (embedding, input_grad[None], grad_up, grad_down, grad_kernel)


def solution(mesh):
    return jax.shard_map(
        on_device,
        mesh=mesh,
        in_specs=(
            P("slide", None, "rows", None),
            P(),
            P(),
            P(),
            P(),
            P(),
            P(),
            P(),
            P(),
            P(),
            P("slide", "rows", None),
            P("slide", None),
            P("slide", "rows", None),
        ),
        out_specs=(P("slide", "rows", None), P("slide", None, "rows", None), P(), P(), P()),
        check_vma=False,
    )
```

```python
import functools
import math

import jax
import jax.numpy as jnp
import numpy as np
from jax import lax
from jax.experimental import pallas as pl
from jax.experimental.pallas import tpu as pltpu
from jax.sharding import PartitionSpec as P

TILE = 32
SLOT = 40
PER = 3
ROWS = 4
MESH = pl.DeviceIdType.MESH
VMEM = pl.BlockSpec(memory_space=pltpu.VMEM)


def greet(peers):
    barrier = pltpu.get_barrier_semaphore()
    for peer in peers:
        pl.semaphore_signal(barrier, inc=1, device_id=peer, device_id_type=MESH)
    pl.semaphore_wait(barrier, len(peers))


def remote(source, target, send, receive, peer, start=True):
    copy = pltpu.make_async_remote_copy(
        src_ref=source,
        dst_ref=target,
        send_sem=send,
        recv_sem=receive,
        device_id=peer,
        device_id_type=MESH,
    )
    if start:
        copy.start()
    return copy


def halo_kernel(count, gathers, head_ref, tail_ref, *refs):
    if gathers:
        block_ref, above_ref, below_ref, all_ref, edge_send, edge_recv, send, recv, own = refs
    else:
        above_ref, below_ref, edge_send, edge_recv = refs
    slide, me = lax.axis_index("slide"), lax.axis_index("rows")
    peers = [(slide, lax.rem(me + k, count)) for k in range(1, count)]
    up, down = peers[-1], peers[0]
    has_up, has_down = me > 0, me < count - 1
    greet(peers if gathers else [up, down])
    downward = remote(tail_ref, above_ref, edge_send.at[0], edge_recv.at[0], down, False)
    upward = remote(head_ref, below_ref, edge_send.at[1], edge_recv.at[1], up, False)
    pl.when(has_down)(downward.start)
    pl.when(has_up)(upward.start)
    if gathers:
        copies = [
            remote(block_ref, all_ref.at[me], send.at[k], recv.at[k], peers[k - 1])
            for k in range(1, count)
        ]
        mine = pltpu.make_async_copy(block_ref, all_ref.at[me], own)
        mine.start()
        mine.wait()
        for copy in copies:
            copy.wait()
    pl.when(has_down)(downward.wait_send)
    pl.when(has_up)(upward.wait_send)
    pl.when(has_up)(downward.wait_recv)
    pl.when(has_down)(upward.wait_recv)


def halo(cells, count, channel_id, block=None):
    channels, height, across = cells.shape
    gathers = block is not None
    turned = cells.transpose(1, 0, 2)
    operands = [turned[:3], turned[height - 3 :]]
    edge = jax.ShapeDtypeStruct((3, channels, across), cells.dtype)
    shapes = [edge, edge]
    scratch = [pltpu.SemaphoreType.DMA((2,)), pltpu.SemaphoreType.DMA((2,))]
    if gathers:
        operands.append(block)
        shapes.append(jax.ShapeDtypeStruct((count,) + block.shape, block.dtype))
        scratch += [
            pltpu.SemaphoreType.DMA((count,)),
            pltpu.SemaphoreType.DMA((count,)),
            pltpu.SemaphoreType.DMA,
        ]
    above, below, *rest = pl.pallas_call(
        functools.partial(halo_kernel, count, gathers),
        out_shape=tuple(shapes),
        in_specs=[VMEM] * len(operands),
        out_specs=(VMEM,) * len(shapes),
        scratch_shapes=scratch,
        compiler_params=pltpu.CompilerParams(collective_id=channel_id, has_side_effects=True),
        name="halo",
    )(*operands)
    me = lax.axis_index("rows")
    above = jnp.where(me > 0, above, jnp.zeros_like(above))
    below = jnp.where(me < count - 1, below, jnp.zeros_like(below))
    spare = jnp.zeros((channels, SLOT - height - 6, across), cells.dtype)
    above, below = above.transpose(1, 0, 2), below.transpose(1, 0, 2)
    return jnp.concatenate([above, cells, below, spare], axis=1), *rest


def sum_kernel(slides, count, part_ref, out_ref, near, half, far, send, recv):
    slide, me = lax.axis_index("slide"), lax.axis_index("rows")
    across = [(lax.rem(slide + k, slides), me) for k in range(1, slides)]
    along = [(slide, lax.rem(me + k, count)) for k in range(1, count)]
    greet(across + along)
    first = [
        remote(part_ref.at[peer[0]], near.at[k], send.at[0, k], recv.at[0, k], peer)
        for k, peer in enumerate(across)
    ]
    for copy in first:
        copy.wait()
    total = part_ref[slide].astype(jnp.float32)
    for k in range(slides - 1):
        total = total + near[k].astype(jnp.float32)
    half[...] = total.astype(jnp.bfloat16)
    second = [
        remote(half.at[peer[1]], far.at[k], send.at[1, k], recv.at[1, k], peer)
        for k, peer in enumerate(along)
    ]
    for copy in second:
        copy.wait()
    total = half[me].astype(jnp.float32)
    for k in range(count - 1):
        total = total + far[k].astype(jnp.float32)
    out_ref[slide, me] = total.astype(jnp.bfloat16)
    third = [
        remote(out_ref.at[slide, me], out_ref.at[slide, me], send.at[2, k], recv.at[2, k], peer)
        for k, peer in enumerate(along)
    ]
    for copy in third:
        copy.wait()
    fourth = [
        remote(out_ref.at[slide], out_ref.at[slide], send.at[3, k], recv.at[3, k], peer)
        for k, peer in enumerate(across)
    ]
    for copy in fourth:
        copy.wait()


def sum_everywhere(rows, slides, count):
    length, across = rows.shape
    share = 16 * pl.cdiv(length, 16 * slides * count)
    padded = jnp.pad(rows, ((0, slides * count * share - length), (0, 0))).astype(jnp.bfloat16)
    shape = (slides, count, share, across)
    totals = pl.pallas_call(
        functools.partial(sum_kernel, slides, count),
        out_shape=jax.ShapeDtypeStruct(shape, jnp.bfloat16),
        in_specs=[VMEM],
        out_specs=VMEM,
        scratch_shapes=[
            pltpu.VMEM((slides - 1,) + shape[1:], jnp.bfloat16),
            pltpu.VMEM(shape[1:], jnp.bfloat16),
            pltpu.VMEM((count - 1,) + shape[2:], jnp.bfloat16),
            pltpu.SemaphoreType.DMA((4, max(slides, count) - 1)),
            pltpu.SemaphoreType.DMA((4, max(slides, count) - 1)),
        ],
        compiler_params=pltpu.CompilerParams(collective_id=2, has_side_effects=True),
        name="sum_everywhere",
    )(padded.reshape(shape))
    return totals.reshape(-1, across)[:length].astype(jnp.float32)


def shifted_stack(rows):
    across = rows.shape[1]
    lane = lax.broadcasted_iota(jnp.int32, rows.shape, 1)
    spare = jnp.zeros((across - PER * SLOT, across), jnp.float32)
    pieces = []
    for b in range(7):
        offset = b - 3
        if offset == 0:
            piece = rows
        else:
            piece = pltpu.roll(rows, (-offset) % across, 1)
            inside = lane < across - offset if offset > 0 else lane >= -offset
            piece = jnp.where(inside, piece, 0.0)
        pieces.append(piece)
        if b % PER == PER - 1:
            pieces.append(spare)
    return jnp.concatenate(pieces, axis=0).astype(jnp.bfloat16)


def banded(taps_ref, c, first, height):
    parts = []
    for g in range(3):
        part = taps_ref[first + g, pl.ds(c, 1), :]
        part = jnp.broadcast_to(part, (height, 128))
        parts.append(pltpu.roll(part, 0, 1, stride=1, stride_axis=0))
    return jnp.concatenate(parts, axis=1)


def diagonal_sums(cells):
    height, across = cells.shape
    total = cells[:8]
    for start in range(8, height, 8):
        total = total + pltpu.roll(cells[start : start + 8], across - start, 1)
    row = lax.broadcasted_iota(jnp.int32, total.shape, 0)
    for bit in (4, 2, 1):
        total = jnp.where((row // bit) % 2 == 1, pltpu.roll(total, across - bit, 1), total)
    return jnp.sum(total, axis=0, keepdims=True)


def forward_kernel(
    ext_ref, taps_ref, channel_ref, up_ref, up_bias, down_ref, mask_ref, branch_ref,
    grad_ref, embed_ref, up_out, down_out, held, sums, hidden_sum, slope_gain,
):
    conv_bias, gain_ref, bias_ref, down_bias = [channel_ref.at[i] for i in range(4)]
    channels, _, across = ext_ref.shape
    height = grad_ref.shape[1]
    hidden_units = up_ref.shape[1]
    depth = 2 * 128 + SLOT

    def conv_channel(c, carry):
        rows = ext_ref[c].astype(jnp.float32)
        stack = shifted_stack(rows)
        hi = banded(taps_ref, c, 0, height)
        lo = banded(taps_ref, channels + c, 0, height)
        left = jnp.concatenate([hi, lo], axis=0).astype(jnp.bfloat16)[:, :depth]
        both = jnp.dot(left, stack, preferred_element_type=jnp.float32)
        held[pl.ds(c, height, stride=channels), :] = both[:height] + both[height:]
        sums[pl.ds(c, 1), :] = jnp.sum(rows, axis=0, keepdims=True) - jnp.sum(
            rows[:3], axis=0, keepdims=True
        ) - jnp.sum(rows[height + 3 :], axis=0, keepdims=True)
        return carry

    lax.fori_loop(0, channels, conv_channel, 0, unroll=8)

    slope_gain[...] = jnp.dot(down_ref[...], branch_ref[...], preferred_element_type=jnp.float32)
    hidden_sum[...] = jnp.zeros_like(hidden_sum)
    up_out[...] = jnp.zeros_like(up_out)

    def pixels(block, carry):
        parts = []
        for r in range(ROWS):
            start = pl.multiple_of((block * ROWS + r) * channels, 8)
            parts.append(held[pl.ds(start, channels), :])
        conv = jnp.concatenate(parts, axis=1) + conv_bias[...]
        average = jnp.mean(conv, axis=0, keepdims=True)
        centered = conv - average
        variance = jnp.mean(centered * centered, axis=0, keepdims=True)
        reciprocal = lax.rsqrt(variance + 1e-06)
        standard = centered * reciprocal
        normed = (standard * gain_ref[...] + bias_ref[...]).astype(jnp.bfloat16)
        act = lax.dot_general(
            up_ref[...], normed, (((0,), (0,)), ((), ())), preferred_element_type=jnp.float32
        )
        act = act + up_bias[...]
        cumulative = 0.5 + 0.5 * lax.erf(act * 0.7071067811865476)
        hidden = (act * cumulative).astype(jnp.bfloat16).astype(jnp.float32)
        total = hidden_sum[...]
        for r in range(ROWS):
            total = total + hidden[:, r * across : (r + 1) * across]
        hidden_sum[...] = total
        density = jnp.exp(-0.5 * act * act) * 0.3989422804014327
        slope = cumulative + act * density
        grad_hidden = jnp.concatenate([slope_gain[...]] * ROWS, axis=1)
        grad_act = (grad_hidden * slope).astype(jnp.bfloat16)
        grad_normed = jnp.dot(up_ref[...], grad_act, preferred_element_type=jnp.float32)
        up_out[...] += lax.dot_general(
            normed, grad_act, (((1,), (1,)), ((), ())), preferred_element_type=jnp.float32
        )
        grad_standard = grad_normed * gain_ref[...]
        first = jnp.mean(grad_standard, axis=0, keepdims=True)
        second = jnp.mean(grad_standard * standard, axis=0, keepdims=True)
        grad_conv = reciprocal * (grad_standard - first - standard * second)
        for r in range(ROWS):
            start = pl.multiple_of((block * ROWS + r) * channels, 8)
            held[pl.ds(start, channels), :] = grad_conv[:, r * across : (r + 1) * across]
        return carry

    lax.fori_loop(0, height // ROWS, pixels, 0)

    total = hidden_sum[...]
    total_hi = total.astype(jnp.bfloat16)
    total_lo = (total - total_hi.astype(jnp.float32)).astype(jnp.bfloat16)
    branch = jnp.zeros((channels, across), jnp.float32)
    down = jnp.zeros((channels, hidden_units), jnp.float32)
    for part in (total_hi, total_lo):
        branch += lax.dot_general(
            down_ref[...], part, (((0,), (0,)), ((), ())), preferred_element_type=jnp.float32
        )
        down += lax.dot_general(
            branch_ref[...], part, (((1,), (1,)), ((), ())), preferred_element_type=jnp.float32
        )
    down_out[...] = down
    embed_ref[...] = sums[...] + mask_ref[...] * (branch + height * down_bias[...])

    def turn(c, carry):
        grad_ref[c] = held[pl.ds(c, height, stride=channels), :].astype(jnp.bfloat16)
        return carry

    lax.fori_loop(0, channels, turn, 0, unroll=8)


def backward_kernel(grad_ref, image_ref, taps_ref, cotangent_ref, out_ref, kernel_ref):
    channels, height, across = image_ref.shape
    depth = 2 * 128 + SLOT

    def channel(c, carry):
        stack = shifted_stack(grad_ref[c].astype(jnp.float32))
        left = banded(taps_ref, c, 3, height).astype(jnp.bfloat16)[:, :depth]
        conv = jnp.dot(left, stack, preferred_element_type=jnp.float32)
        out_ref[c] = (conv + cotangent_ref[pl.ds(c, 1), :]).astype(jnp.bfloat16)
        spare = jnp.zeros((3 * 128 - depth, across), jnp.bfloat16)
        cross = lax.dot_general(
            image_ref[c],
            jnp.concatenate([stack, spare], axis=0),
            (((1,), (1,)), ((), ())),
            preferred_element_type=jnp.float32,
        )
        for g in range(3):
            kernel_ref[g, pl.ds(c, 1), :] = diagonal_sums(cross[:, g * 128 : (g + 1) * 128])
        return carry

    lax.fori_loop(0, channels, channel, 0, unroll=8)


def tap_lanes_of(mirrored):
    places = np.zeros((49, 3 * 128), np.float32)
    for a in range(7):
        for b in range(7):
            tap = 7 * (6 - a) + 6 - b if mirrored else 7 * a + b
            places[tap, 128 * (b // PER) + SLOT * (b % PER) + a] = 1.0
    return places


def taps_of(rows):
    channels = rows.shape[1]
    groups = rows[:, :, : PER * SLOT].transpose(1, 0, 2).reshape(channels, 9, SLOT)
    return groups[:, :7, :7].transpose(0, 2, 1)


def on_device(
    features,
    depth_kernel,
    depth_bias,
    norm_gain,
    norm_bias,
    up_weight,
    up_bias,
    down_weight,
    down_bias,
    layer_scale,
    tissue,
    aggregator_order,
    tile_cotangent,
):
    image = features[0]
    channels, height, across = image.shape
    tiles_here = across // TILE
    hidden_units = up_weight.shape[1]
    taps_hi = lax.reduce_precision(depth_kernel, 8, 7)
    taps_lo = depth_kernel - taps_hi
    both = jnp.concatenate([taps_hi, taps_lo], axis=0).astype(jnp.bfloat16)
    places = np.concatenate([tap_lanes_of(False), tap_lanes_of(True)], axis=1)
    places = places.reshape(49, 6, 128).transpose(1, 0, 2)
    rows = lax.dot_general(
        jnp.broadcast_to(both, (6,) + both.shape),
        jnp.asarray(places, jnp.bfloat16),
        (((2,), (1,)), ((0,), (0,))),
        preferred_element_type=jnp.float32,
    )
    slides, count = lax.axis_size("slide"), lax.axis_size("rows")
    extended, gathered = halo(image, count, 0, tile_cotangent[0])
    gathered = gathered.reshape(count * tiles_here, channels)
    positions = lax.dynamic_slice_in_dim(
        aggregator_order[0], lax.axis_index("rows") * tiles_here, tiles_here
    )
    wanted = jnp.take(gathered, positions, axis=0).astype(jnp.float32)
    cotangent = jnp.repeat(wanted.T, TILE, axis=1)
    mask = jnp.repeat(tissue[0, 0].astype(jnp.float32), TILE)
    scaled_mask = mask[None, :] * layer_scale[:, None]
    grad_branch = (scaled_mask * cotangent).astype(jnp.bfloat16)
    f32 = jnp.float32
    grad_conv, embed, up_term, down_term = pl.pallas_call(
        forward_kernel,
        out_shape=(
            jax.ShapeDtypeStruct((channels, height, across), jnp.bfloat16),
            jax.ShapeDtypeStruct((channels, across), f32),
            jax.ShapeDtypeStruct((channels, hidden_units), f32),
            jax.ShapeDtypeStruct((channels, hidden_units), f32),
        ),
        in_specs=[VMEM] * 8,
        out_specs=(VMEM,) * 4,
        scratch_shapes=[
            pltpu.VMEM((height * channels, across), f32),
            pltpu.VMEM((channels, across), f32),
            pltpu.VMEM((hidden_units, across), f32),
            pltpu.VMEM((hidden_units, across), f32),
        ],
        compiler_params=pltpu.CompilerParams(vmem_limit_bytes=56 * 1024 * 1024),
        name="forward_block",
    )(
        extended,
        rows,
        jnp.stack([depth_bias, norm_gain, norm_bias, down_bias])[:, :, None],
        up_weight,
        up_bias[:, None],
        down_weight,
        scaled_mask,
        grad_branch,
    )
    embedding = (
        embed.reshape(channels, tiles_here, TILE).sum(axis=2) / (height * TILE)
    ).T[None]
    (grad_extended,) = halo(grad_conv, count, 1)
    input_grad, kernel_rows = pl.pallas_call(
        backward_kernel,
        out_shape=(
            jax.ShapeDtypeStruct((channels, height, across), jnp.bfloat16),
            jax.ShapeDtypeStruct((3, channels, 128), f32),
        ),
        in_specs=[VMEM] * 4,
        out_specs=(VMEM,) * 2,
        compiler_params=pltpu.CompilerParams(vmem_limit_bytes=40 * 1024 * 1024),
        name="backward_conv",
    )(grad_extended, image, rows, cotangent)
    kernel_term = taps_of(kernel_rows)[:, ::-1, ::-1].reshape(channels, 49)
    loss_norm = 1.0 / math.sqrt(slides * count * height * across)
    tap_lanes = kernel_term.shape[1]
    wide = jnp.pad(kernel_term, ((0, 0), (0, across - tap_lanes)))
    blocks = hidden_units // across
    combined = jnp.concatenate(
        [
            up_term.reshape(channels, blocks, across).transpose(1, 0, 2),
            down_term.reshape(channels, blocks, across).transpose(1, 0, 2),
            wide[None],
        ],
        axis=0,
    )
    totals = sum_everywhere((combined * loss_norm).reshape(-1, across), slides, count)
    totals = totals.reshape(2 * blocks + 1, channels, across)
    grad_up = totals[:blocks].transpose(1, 0, 2).reshape(channels, hidden_units)
    grad_down = totals[blocks : 2 * blocks].transpose(0, 2, 1).reshape(hidden_units, channels)
    grad_kernel = totals[2 * blocks, :, :tap_lanes]
    return (embedding, input_grad[None], grad_up, grad_down, grad_kernel)


def solution(mesh):
    return jax.shard_map(
        on_device,
        mesh=mesh,
        in_specs=(
            P("slide", None, "rows", None),
            P(),
            P(),
            P(),
            P(),
            P(),
            P(),
            P(),
            P(),
            P(),
            P("slide", "rows", None),
            P("slide", None),
            P("slide", "rows", None),
        ),
        out_specs=(P("slide", "rows", None), P("slide", None, "rows", None), P(), P(), P()),
        check_vma=False,
    )
```
